32 devices in a mesh: groups: 2 (over y), feat: 4 (over z), layer: 2 (over x), tok: 2 (over core).
Axes of the slice: x: 2, y: 2, z: 4, core: 2. Of those that a mesh axis runs over, the one named last changes fastest.
Arguments:
- residual_in: float32 [256, 2, 1792], P('groups', 'tok', 'feat'), parts along dimension 0, may hold values from -6 to 6
- attn_scale: float32 [2, 256], P('layer', 'groups'), parts along dimension 1, may hold values from 0.4 to 2.5
- mlp_scale: float32 [2, 256], P('layer', 'groups'), parts along dimension 1, may hold values from 0.4 to 2.5
- patterns: bfloat16 [2, 8, 4, 64, 64], P('layer', None, 'groups'), parts along dimension 2, may hold values from 0.0029907227 to 0.059814453
- lengths: int32 [4], P('groups'), parts along dimension 0, may hold values from 16 to 64
- value_proj: bfloat16 [2, 2, 1792, 1024], P('layer', 'tok', None, 'feat'), may hold values from -0.09375 to 0.09375
- out_proj: bfloat16 [2, 4, 256, 2, 2, 1792], P('layer', None, None, None, 'tok', 'feat'), may hold values from -0.125 to 0.125
- enc_weight: bfloat16 [2, 2, 1792, 512], P('layer', 'tok', None, 'feat'), may hold values from -0.09375 to 0.09375
- enc_bias: float32 [2, 512], P('layer', 'feat'), may hold values from -3 to 3
- dec_weight: bfloat16 [2, 2, 512, 2, 1792], P('layer', None, None, 'tok', 'feat'), may hold values from -0.25 to 0.25
- errors: float32 [2, 256, 2, 1792], P('layer', 'groups', 'tok', 'feat'), parts along dimension 1, may hold values from -4 to 4
- clamp_mode: int32 [2, 16384], P('layer', 'feat'), may hold values from 0 to 2
- clamp_index: int32 [2, 16384], P('layer', 'feat'), may hold values from 0 to 63
- clamp_values: float32 [64], replicated, may hold values from 0.25 to 3
- active_blocks: int32 [2, 4], P('layer', 'feat'), may hold values from 0 to 31
Outputs:
- residual_out: float32 [2, 256, 2, 1792], P('layer', 'groups', 'tok', 'feat'), parts along dimension 1
- features: bfloat16 [2, 256, 512], P('layer', 'groups', 'feat'), parts along dimension 1
The draws below stay inside these ranges and needn't reach their ends.
There are 2 independent parts, one for each index of `groups`. The reference program is written for one: setup_inputs(seed, part) draws one part's arguments, and reference() takes and returns one part's arrays. A program takes and returns all parts, laid end to end along the dimension named above; an argument that names none is the same for every part. Nothing has to cross between parts.
Inputs may be any that keep to these rules, and one draw needn't show every extreme that they name: `clamp_mode`: 0 leaves a feature free, 1 sets it to its table value, 2 multiplies it by its table value. `lengths`: positions at or past a prompt's length are padding.
All inputs are finite; a program needn't handle non-finite values.
Results may differ from the reference program's by a relative error of at most 0.018.
Values may be sent and summed in bfloat16 or wider, within the bound.
A program may use at most 64 MiB of HBM per device.

```python
import math
import jax
import jax.numpy as jnp

D = 3584
HD = 256
HEADS = 8
KVH = 4
FEATURES = 16384
BLOCK = 128
VALUES = 64
SEQ = 64
PROMPTS = 2
QPK = 2
LAYERS = 2
RANGES = 4
ACT = 512
SHARD_BLOCKS = 32
SLABS = 2
SLAB = 1792
ROWS = 128


def place_ends(values, stream_key, low, high):
    spot = [jax.random.randint(jax.random.fold_in(stream_key, axis), (), 0, length) for axis, length in enumerate(values.shape)]
    widest = values.shape.index(max(values.shape))
    neighbour = spot[:widest] + [(spot[widest] + 1) % values.shape[widest]] + spot[widest + 1:]
    return values.at[tuple(spot)].set(low).at[tuple(neighbour)].set(high)


def level_of(key, shape, pieces, smallest, top_value):
    def one(axis_at, shards_of):
        draws = jax.random.uniform(jax.random.fold_in(jax.random.fold_in(key, 6), axis_at), (shards_of,), jnp.float32, smallest / len(pieces), top_value / len(pieces))
        return jnp.repeat(jnp.exp(draws), shape[axis_at] // shards_of).reshape((-1,) + (1,) * (len(shape) - axis_at - 1))

    factor_of = one(*pieces[0])
    for cut in pieces[1:]:
        factor_of = factor_of * one(*cut)
    return factor_of


def normal_values(own_key, shape, scale, limit, cuts=(), kind=jnp.bfloat16):
    values = jax.random.normal(own_key, shape, jnp.float32) * scale
    if len(cuts) > 0:
        values = level_of(own_key, shape, cuts, -0.22, 0.18) * values
    return jnp.clip(values, min=-limit, max=limit).astype(kind)


def setup_inputs(seed: int = 0, part: int = 0) -> dict:
    keys = jax.random.split(jax.random.key(seed), 16)
    own_keys = jax.random.split(jax.random.fold_in(keys[15], part), 16)
    return {
        "residual_in": normal_values(own_keys[0], (ROWS, SLABS, SLAB), 1.0, 6.0, ((1, 2), (2, 4)), jnp.float32),
        "attn_scale": jnp.clip(jnp.exp(math.log(2.5) - 1.8325814 * jax.random.uniform(own_keys[1], (LAYERS, ROWS), jnp.float32) ** level_of(own_keys[1], (LAYERS, ROWS), ((0, 2),), -0.2, 0.2)), 0.4, 2.5),
        "mlp_scale": jnp.clip(jnp.exp(math.log(2.5) - 1.8325814 * jax.random.uniform(own_keys[2], (LAYERS, ROWS), jnp.float32) ** level_of(own_keys[2], (LAYERS, ROWS), ((0, 2),), -0.2, 0.2)), 0.4, 2.5),
        "patterns": jnp.clip(jnp.exp(math.log(0.059814453) - 2.9957323 * jax.random.uniform(own_keys[3], (LAYERS, HEADS, PROMPTS, SEQ, SEQ), jnp.float32) ** level_of(own_keys[3], (LAYERS, HEADS, PROMPTS, SEQ, SEQ), ((0, 2),), -0.2, 0.2)), 0.0029907227, 0.059814453).astype(jnp.bfloat16),
        "lengths": jax.random.randint(own_keys[4], (PROMPTS,), SEQ // 4, SEQ + 1).astype(jnp.int32),
        "value_proj": normal_values(keys[5], (LAYERS, SLABS, SLAB, KVH * HD), D ** -0.5, 0.09375, ((0, 2), (1, 2), (3, 4))),
        "out_proj": normal_values(keys[6], (LAYERS, KVH, HD, QPK, SLABS, SLAB), (HEADS * HD) ** -0.5, 0.125, ((0, 2), (4, 2), (5, 4))),
        "enc_weight": normal_values(keys[7], (LAYERS, SLABS, SLAB, ACT), D ** -0.5, 0.09375, ((0, 2), (1, 2), (3, 4))),
        "enc_bias": normal_values(keys[8], (LAYERS, ACT), 0.5, 3.0, ((0, 2), (1, 4)), jnp.float32),
        "dec_weight": normal_values(keys[9], (LAYERS, LAYERS, ACT, SLABS, SLAB), ACT ** -0.5, 0.25, ((0, 2), (3, 2), (4, 4))),
        "errors": normal_values(own_keys[10], (LAYERS, ROWS, SLABS, SLAB), 0.5, 4.0, ((0, 2), (2, 2), (3, 4)), jnp.float32),
        "clamp_mode": place_ends(jax.random.randint(keys[11], (LAYERS, FEATURES), 0, 3), jax.random.fold_in(keys[11], 1), 0, 2).astype(jnp.int32),
        "clamp_index": place_ends(jax.random.randint(keys[12], (LAYERS, FEATURES), 0, VALUES), jax.random.fold_in(keys[12], 1), 0, VALUES - 1).astype(jnp.int32),
        "clamp_values": jnp.clip(jax.random.uniform(keys[13], (VALUES,), jnp.float32, 0.25, 3.0), 0.25, 3.0),
        "active_blocks": place_ends(jax.random.randint(keys[14], (LAYERS, RANGES), 0, SHARD_BLOCKS), jax.random.fold_in(keys[14], 1), 0, SHARD_BLOCKS - 1).astype(jnp.int32),
    }


def pick_block(lookup_table, chosen):
    shaped = lookup_table.reshape(RANGES, SHARD_BLOCKS, BLOCK)
    taken = jnp.take_along_axis(shaped, chosen.astype(jnp.int32)[:, None, None], axis=1)
    return taken[:, 0, :].reshape(ACT)


def reference(residual_in, attn_scale, mlp_scale, patterns, lengths, value_proj, out_proj, enc_weight, enc_bias, dec_weight, errors, clamp_mode, clamp_index, clamp_values, active_blocks):
    positions = jnp.arange(SEQ, dtype=jnp.int32)
    live_rows = (positions[None, :] < lengths[:, None]).reshape(ROWS)
    keep_keys = (positions[None, None, :] <= positions[None, :, None]) & (positions[None, None, :] < lengths[:, None, None])
    state = residual_in.reshape(ROWS, D)
    feature_list = []
    state_list = []
    for layer_num in range(LAYERS):
        normed = (state * attn_scale[layer_num][:, None]).astype(jnp.bfloat16)
        values = jnp.dot(normed, value_proj[layer_num].reshape(D, KVH * HD), preferred_element_type=jnp.float32).astype(jnp.bfloat16)
        value_grid = values.reshape(PROMPTS, SEQ, KVH, HD).astype(jnp.float32)
        pattern_grid = jnp.where(keep_keys[None], patterns[layer_num].astype(jnp.float32), 0.0).reshape(KVH, QPK, PROMPTS, SEQ, SEQ)
        head_out = jnp.einsum("gupqk,pkgd->pqgdu", pattern_grid, value_grid).astype(jnp.bfloat16).reshape(ROWS, KVH * HD * QPK)
        attention = jnp.dot(head_out, out_proj[layer_num].reshape(KVH * HD * QPK, D), preferred_element_type=jnp.float32)
        middle = state + attention
        normed_mlp = (middle * mlp_scale[layer_num][:, None]).astype(jnp.bfloat16)
        preact = jnp.dot(normed_mlp, enc_weight[layer_num].reshape(D, ACT), preferred_element_type=jnp.float32) + enc_bias[layer_num]
        active = jnp.maximum(preact, 0.0)
        modes = pick_block(clamp_mode[layer_num], active_blocks[layer_num])
        levels = clamp_values[pick_block(clamp_index[layer_num], active_blocks[layer_num])]
        clamped = jnp.where(modes == 1, levels, jnp.where(modes == 2, active * levels, active))
        features = jnp.where(live_rows[:, None], clamped, 0.0).astype(jnp.bfloat16)
        feature_list.append(features)
        recon = jnp.zeros((ROWS, D), jnp.float32)
        for source_num in range(layer_num + 1):
            recon = recon + jnp.dot(feature_list[source_num], dec_weight[source_num, layer_num].reshape(ACT, D), preferred_element_type=jnp.float32)
        state = middle + recon + errors[layer_num].reshape(ROWS, D)
        state_list.append(state)
    return jnp.stack(state_list).reshape(LAYERS, ROWS, SLABS, SLAB), jnp.stack(feature_list)
```

```python
import functools

import jax
import jax.numpy as jnp
from jax import lax
from jax.experimental import pallas as pl
from jax.experimental.pallas import tpu as pltpu
from jax.sharding import PartitionSpec as P

F32 = jnp.float32
BF16 = jnp.bfloat16
NT = (((1,), (1,)), ((), ()))


def column(row):
    rows = row.shape[1]
    return jnp.transpose(jnp.broadcast_to(row, (128, rows)))[:, 0:1]


def kernel(
    sizes,
    lengths, table, chosen,
    scale_attn, scale_mlp, bias, mode_row, index_row,
    x_in, err_in, pat_in, wv_in, wo_in, we_in, wd_in,
    out_ref, feat_ref,
    x_t, err_t, pat, wv, wo, we, wd,
    xbuf, slots, slots2, vals, feats, part_v, part_v2, part_e, part_e2,
    next_scale, nbuf, xsend, acc_in, acc_out, att,
    local_sem, xs_send, xs_recv, ns_send, v_send, v_recv, m_send, m_recv,
    f_send, f_recv, t_send, t_recv, one_send, one_recv, a_send, a_recv,
):
    layers, feat_n, seq, prompts, head_dim, per_group, kv, width, block, rows, entries = sizes
    me_l = lax.axis_index("layer")
    me_f = lax.axis_index("feat")
    me_t = lax.axis_index("tok")
    has_next = me_l < layers - 1
    has_prev = me_l > 0
    other = 1 - me_t
    nxt = jnp.minimum(me_l + 1, layers - 1)
    prv = jnp.maximum(me_l - 1, 0)

    loads = [
        pltpu.make_async_copy(src, dst, local_sem.at[i])
        for i, (src, dst) in enumerate(
            ((x_in, x_t), (wv_in, wv), (pat_in, pat), (wo_in, wo), (we_in, we), (wd_in, wd), (err_in, err_t))
        )
    ]
    for load in loads:
        load.start()
    l_x, l_wv, l_pat, l_wo, l_we, l_wd, l_err = loads

    barrier = pltpu.get_barrier_semaphore()
    pl.semaphore_signal(barrier, inc=1, device_id={"tok": other}, device_id_type=pl.DeviceIdType.MESH)
    for j in range(1, feat_n):
        pl.semaphore_signal(
            barrier, inc=1, device_id={"feat": (me_f + j) % feat_n}, device_id_type=pl.DeviceIdType.MESH
        )

    @pl.when(has_next)
    def _():
        for s in range(feat_n):
            pl.semaphore_signal(
                barrier, inc=1, device_id={"layer": nxt, "feat": s}, device_id_type=pl.DeviceIdType.MESH
            )

    @pl.when(has_prev)
    def _():
        for s in range(feat_n):
            pl.semaphore_signal(
                barrier, inc=1, device_id={"layer": prv, "feat": s}, device_id_type=pl.DeviceIdType.MESH
            )

    def send(src, dst, ss, rs, where):
        return pltpu.make_async_remote_copy(
            src_ref=src, dst_ref=dst, send_sem=ss, recv_sem=rs, device_id=where,
            device_id_type=pl.DeviceIdType.MESH,
        )

    ids = lax.broadcasted_iota(jnp.int32, (rows, 1), 0)
    limit = jnp.zeros((rows, 1), jnp.int32)
    for p in range(prompts):
        limit = jnp.where(ids // seq == p, lengths[p], limit)
    live = ids % seq < limit
    which = jnp.zeros((1, block), jnp.int32) + chosen[0, 0]
    modes = picks = jnp.zeros((1, block), jnp.int32)
    for b in range(mode_row.shape[1] // block):
        here = which == b
        modes = jnp.where(here, mode_row[:, b * block : (b + 1) * block], modes)
        picks = jnp.where(here, index_row[:, b * block : (b + 1) * block], picks)
    levels = jnp.zeros((1, block), F32)
    for v in range(entries):
        levels = jnp.where(picks == v, table[v], levels)
    mlp_col = column(scale_mlp[...])
    shift = bias[...]

    l_x.wait()
    normed_t = x_t[...] * scale_attn[...]

    @pl.when(jnp.logical_not(has_prev))
    def _():
        slots[me_f] = jnp.transpose(normed_t).astype(BF16)

    neighbours = 1 + jnp.minimum(me_l, 1) + jnp.minimum(layers - 1 - me_l, 1)
    pl.semaphore_wait(barrier, feat_n * neighbours)

    def to_peers(ref, ss, rs):
        copies = [
            send(ref.at[me_f], ref.at[me_f], ss.at[j], rs.at[me_f], {"feat": (me_f + j) % feat_n})
            for j in range(1, feat_n)
        ]
        for copy in copies:
            copy.start()
        return copies

    def arrived(ref, ss, rs, s):
        send(ref.at[s], ref.at[s], ss.at[0], rs.at[s], {"tok": other}).wait_recv()

    def await_peer(ref, ss, rs, s):
        @pl.when(me_f != s)
        def _():
            arrived(ref, ss, rs, s)

    @pl.when(jnp.logical_not(has_prev))
    def _():
        to_peers(slots, xs_send, xs_recv)
        xbuf[...] = jnp.transpose(x_t[...])

    scale_up = send(scale_attn, next_scale, one_send.at[0], one_recv.at[0], {"layer": prv})
    x_up = send(xsend, xbuf, one_send.at[1], one_recv.at[1], {"layer": nxt})

    @pl.when(has_prev)
    def _():
        scale_up.start()

    l_wv.wait()
    acc = jnp.zeros((rows, kv), F32)
    part_v[...] = acc
    for s in range(feat_n):
        @pl.when(jnp.logical_or(has_prev, me_f != s))
        def _():
            arrived(slots, xs_send, xs_recv, s)

        part_v[...] += jnp.dot(slots[s], wv[pl.ds(s * width, width), :], preferred_element_type=F32)
    tok_v = send(part_v, part_v2, t_send.at[0], t_recv.at[0], {"tok": other})
    tok_v.start()
    tok_v.wait_recv()
    vals[me_f] = (part_v[...] + part_v2[...]).astype(BF16)
    v_copies = to_peers(vals, v_send, v_recv)

    l_pat.wait()
    l_wo.wait()
    q_ids = lax.broadcasted_iota(jnp.int32, (seq, seq), 0)
    k_ids = lax.broadcasted_iota(jnp.int32, (seq, seq), 1)
    keeps = [jnp.logical_and(k_ids <= q_ids, k_ids < lengths[p]) for p in range(prompts)]
    att[...] = jnp.zeros((rows, width), F32)
    for s in range(feat_n):
        await_peer(vals, v_send, v_recv, s)
        group = s * kv // head_dim
        d0 = s * kv % head_dim
        total = att[...]
        for u in range(per_group):
            heads = []
            for p in range(prompts):
                weights = jnp.where(keeps[p], pat[group * per_group + u, p].astype(F32), 0.0).astype(BF16)
                heads.append(
                    jnp.dot(weights, vals[s, pl.ds(p * seq, seq), :], preferred_element_type=F32).astype(BF16)
                )
            head = jnp.concatenate(heads, axis=0)
            total = total + lax.dot_general(
                head, wo[group, u, :, pl.ds(d0, kv)], NT, preferred_element_type=F32
            )
        att[...] = total

    @pl.when(has_prev)
    def _():
        x_up.wait_recv()

    middle = xbuf[...] + att[...]
    att[...] = middle
    slots2[me_f] = (middle * mlp_col).astype(BF16)
    m_copies = to_peers(slots2, m_send, m_recv)
    l_we.wait()
    part_e[...] = jnp.zeros((rows, block), F32)
    for s in range(feat_n):
        await_peer(slots2, m_send, m_recv, s)
        part_e[...] += jnp.dot(slots2[s], we[pl.ds(s * width, width), :], preferred_element_type=F32)
    tok_e = send(part_e, part_e2, t_send.at[1], t_recv.at[1], {"tok": other})
    tok_e.start()
    tok_e.wait_recv()
    preact = part_e[...] + part_e2[...] + shift
    active = jnp.maximum(preact, 0.0)
    clamped = jnp.where(modes == 1, levels, jnp.where(modes == 2, active * levels, active))
    new_feats = jnp.where(live, clamped, 0.0).astype(BF16)
    feats[me_f] = new_feats
    f_copies = to_peers(feats, f_send, f_recv)
    feat_ref[...] = new_feats

    l_err.wait()
    l_wd.wait()
    att[...] += jnp.transpose(err_t[...])

    def acc_copy(t):
        return send(acc_out.at[t], acc_in.at[t], a_send.at[t], a_recv.at[t], {"layer": nxt})

    @pl.when(has_prev)
    def _():
        for t in range(1, layers):
            @pl.when(t >= me_l)
            def _():
                acc_copy(t).wait_recv()
        att[...] += acc_in[me_l]

    for s in range(feat_n):
        await_peer(feats, f_send, f_recv, s)
        att[...] += lax.dot_general(
            feats[s], wd[me_l, :, pl.ds(s * block, block)], NT, preferred_element_type=F32
        )

    norm_up = [
        send(nbuf, slots.at[me_f], ns_send.at[s], xs_recv.at[me_f], {"layer": nxt, "feat": s})
        for s in range(feat_n)
    ]

    @pl.when(has_next)
    def _():
        send(scale_attn, next_scale, one_send.at[0], one_recv.at[0], {"layer": nxt}).wait_recv()
        after = att[...]
        nbuf[...] = (after * column(next_scale[...])).astype(BF16)
        for copy in norm_up:
            copy.start()
        xsend[...] = after
        x_up.start()
        for t in range(1, layers):
            @pl.when(t > me_l)
            def _():
                total = jnp.zeros((rows, width), F32)
                for s in range(feat_n):
                    total += lax.dot_general(
                        feats[s], wd[t, :, pl.ds(s * block, block)], NT, preferred_element_type=F32
                    )
                acc_out[t] = total

                @pl.when(has_prev)
                def _():
                    acc_out[t] += acc_in[t]

                acc_copy(t).start()

    out_ref[...] = jnp.transpose(att[...])

    @pl.when(jnp.logical_not(has_prev))
    def _():
        for j in range(1, feat_n):
            send(slots.at[me_f], slots.at[me_f], xs_send.at[j], xs_recv.at[me_f], {"tok": other}).wait_send()

    @pl.when(has_prev)
    def _():
        scale_up.wait_send()

    tok_v.wait_send()
    tok_e.wait_send()
    for copy in v_copies + m_copies + f_copies:
        copy.wait_send()

    @pl.when(has_next)
    def _():
        for copy in norm_up:
            copy.wait_send()
        x_up.wait_send()
        for t in range(1, layers):
            @pl.when(t > me_l)
            def _():
                acc_copy(t).wait_send()


def local(
    residual_in, attn_scale, mlp_scale, patterns, lengths, value_proj, out_proj, enc_weight, enc_bias,
    dec_weight, errors, clamp_mode, clamp_index, clamp_values, active_blocks,
):
    layers = lax.axis_size("layer")
    feat_n = lax.axis_size("feat")
    prompts, seq = patterns.shape[2], patterns.shape[3]
    head_dim, per_group = out_proj.shape[2], out_proj.shape[3]
    kv = value_proj.shape[3]
    rows, _, width = residual_in.shape
    block = enc_bias.shape[1]
    entries = clamp_values.shape[0]
    sizes = (layers, feat_n, seq, prompts, head_dim, per_group, kv, width, block, rows, entries)
    x_in = residual_in[:, 0, :].T
    err_in = errors[0, :, 0, :].T
    pat_in = patterns[0]
    wv_in = value_proj[0, 0]
    wo_in = jnp.transpose(out_proj[0, :, :, :, 0, :], (0, 2, 3, 1))
    we_in = enc_weight[0, 0]
    wd_in = jnp.transpose(dec_weight[0, :, :, 0, :], (0, 2, 1))
    smem = pl.BlockSpec(memory_space=pltpu.SMEM)
    vmem = pl.BlockSpec(memory_space=pltpu.VMEM)
    hbm = pl.BlockSpec(memory_space=pl.ANY)
    big = (x_in, err_in, pat_in, wv_in, wo_in, we_in, wd_in)
    dma = pltpu.SemaphoreType.DMA
    out_t, out_f = pl.pallas_call(
        functools.partial(kernel, sizes),
        out_shape=(
            jax.ShapeDtypeStruct((width, rows), F32),
            jax.ShapeDtypeStruct((rows, block), BF16),
        ),
        in_specs=[smem] * 3 + [vmem] * 5 + [hbm] * 7,
        out_specs=(vmem, vmem),
        scratch_shapes=[pltpu.VMEM(a.shape, a.dtype) for a in big]
        + [
            pltpu.VMEM((rows, width), F32),
            pltpu.VMEM((feat_n, rows, width), BF16),
            pltpu.VMEM((feat_n, rows, width), BF16),
            pltpu.VMEM((feat_n, rows, kv), BF16),
            pltpu.VMEM((feat_n, rows, block), BF16),
            pltpu.VMEM((rows, kv), F32),
            pltpu.VMEM((rows, kv), F32),
            pltpu.VMEM((rows, block), F32),
            pltpu.VMEM((rows, block), F32),
            pltpu.VMEM((1, rows), F32),
            pltpu.VMEM((rows, width), BF16),
            pltpu.VMEM((rows, width), F32),
            pltpu.VMEM((layers, rows, width), F32),
            pltpu.VMEM((layers, rows, width), F32),
            pltpu.VMEM((rows, width), F32),
            dma((7,)),
        ]
        + [dma((feat_n,))] * 9
        + [dma((2,))] * 4
        + [dma((layers,))] * 2,
        compiler_params=pltpu.CompilerParams(collective_id=0, has_side_effects=True),
    )(lengths, clamp_values, active_blocks, attn_scale, mlp_scale, enc_bias, clamp_mode, clamp_index, *big)
    return out_t.T[None, :, None, :], out_f[None]


def solution(mesh):
    return jax.shard_map(
        local,
        mesh=mesh,
        in_specs=(
            P("groups", "tok", "feat"),
            P("layer", "groups"),
            P("layer", "groups"),
            P("layer", None, "groups", None, None),
            P("groups"),
            P("layer", "tok", None, "feat"),
            P("layer", None, None, None, "tok", "feat"),
            P("layer", "tok", None, "feat"),
            P("layer", "feat"),
            P("layer", None, None, "tok", "feat"),
            P("layer", "groups", "tok", "feat"),
            P("layer", "feat"),
            P("layer", "feat"),
            P(),
            P("layer", "feat"),
        ),
        out_specs=(P("layer", "groups", "tok", "feat"), P("layer", "groups", "feat")),
        check_vma=False,
    )
```

```python
import functools

import jax
import jax.numpy as jnp
from jax import lax
from jax.experimental import pallas as pl
from jax.experimental.pallas import tpu as pltpu
from jax.sharding import PartitionSpec as P

F32 = jnp.float32
BF16 = jnp.bfloat16
NT = (((1,), (1,)), ((), ()))


def column(row):
    rows = row.shape[1]
    return jnp.transpose(jnp.broadcast_to(row, (128, rows)))[:, 0:1]


def kernel(
    sizes,
    lengths, table, chosen,
    scale_attn, scale_mlp, bias, mode_row, index_row,
    x_in, err_in, pat_in, wv_in, wo_in, we_in, wd_in,
    out_ref, feat_ref,
    x_t, err_t, pat, wv, wo, we, wd,
    xbuf, slots, vals, feats, part_v, part_v2, part_e, part_e2, e_out, e_in,
    next_scale, nbuf, xsend, acc_in, acc_out, att, err, wek, relay_in, relay_mid,
    local_sem, xs_send, xs_recv, ns_send, v_send, v_recv, m_send, m_recv, f_send, f_recv,
    t_send, t_recv, up_send, up_recv, one_send, one_recv, a_send, a_recv,
    w_send, w_recv,
):
    layers, feat_n, seq, prompts, head_dim, per_group, kv, width, block, rows, entries = sizes
    me_l = lax.axis_index("layer")
    me_f = lax.axis_index("feat")
    me_t = lax.axis_index("tok")
    has_next = me_l < layers - 1
    has_prev = me_l > 0
    is_first = jnp.logical_not(has_prev)
    other = 1 - me_t
    nxt = jnp.minimum(me_l + 1, layers - 1)
    prv = jnp.maximum(me_l - 1, 0)
    streams = range(prompts)

    loads = [
        pltpu.make_async_copy(src, dst, local_sem.at[i])
        for i, (src, dst) in enumerate(
            ((x_in, x_t), (we_in, we), (wv_in, wv), (pat_in, pat), (wo_in, wo), (wd_in, wd), (err_in, err_t))
        )
    ]
    for load in loads:
        load.start()
    l_x, l_we, l_wv, l_pat, l_wo, l_wd, l_err = loads

    barrier = pltpu.get_barrier_semaphore()
    mesh_id = pl.DeviceIdType.MESH
    pl.semaphore_signal(barrier, inc=1, device_id={"tok": other}, device_id_type=mesh_id)
    for j in range(1, feat_n):
        pl.semaphore_signal(barrier, inc=1, device_id={"feat": (me_f + j) % feat_n}, device_id_type=mesh_id)

    @pl.when(has_next)
    def _():
        for s in range(feat_n):
            pl.semaphore_signal(barrier, inc=1, device_id={"layer": nxt, "feat": s}, device_id_type=mesh_id)

    @pl.when(has_prev)
    def _():
        for s in range(feat_n):
            pl.semaphore_signal(barrier, inc=1, device_id={"layer": prv, "feat": s}, device_id_type=mesh_id)

    def send(src, dst, ss, rs, where):
        return pltpu.make_async_remote_copy(
            src_ref=src, dst_ref=dst, send_sem=ss, recv_sem=rs, device_id=where, device_id_type=mesh_id
        )

    def peer(j):
        return (me_f + j) % feat_n

    def part(p):
        return pl.ds(p * seq, seq)

    l_x.wait()
    x_rows = jnp.transpose(x_t[...])
    normed = (x_rows * column(scale_attn[...])).astype(BF16)

    @pl.when(is_first)
    def _():
        for p in streams:
            slots[p, me_f] = normed[p * seq : (p + 1) * seq]
            xbuf[p] = x_rows[p * seq : (p + 1) * seq]

    neighbours = 1 + jnp.minimum(me_l, 1) + jnp.minimum(layers - 1 - me_l, 1)
    pl.semaphore_wait(barrier, feat_n * neighbours)

    def to_peers(ref, ss, rs, p):
        copies = [
            send(ref.at[p, me_f], ref.at[p, me_f], ss.at[p, j], rs.at[p, me_f], {"feat": peer(j)})
            for j in range(1, feat_n)
        ]
        for copy in copies:
            copy.start()
        return copies

    def arrived(ref, ss, rs, p, s):
        send(ref.at[p, s], ref.at[p, s], ss.at[p, 0], rs.at[p, s], {"tok": other}).wait_recv()

    def await_peer(ref, ss, rs, p, s):
        @pl.when(me_f != s)
        def _():
            arrived(ref, ss, rs, p, s)

    @pl.when(is_first)
    def _():
        for p in streams:
            to_peers(slots, xs_send, xs_recv, p)

    scale_up = send(scale_attn, next_scale, one_send.at[0], one_recv.at[0], {"layer": prv})
    x_up = [send(xsend.at[p], xbuf.at[p], up_send.at[p], up_recv.at[p], {"layer": nxt}) for p in streams]

    @pl.when(has_prev)
    def _():
        scale_up.start()

    def we_rows(s):
        return we.at[pl.ds(pl.multiple_of(s * width, 16), width)]

    l_we.wait()
    own_rows = pltpu.make_async_copy(we_rows(me_f), wek.at[me_f], local_sem.at[7])
    own_rows.start()
    first_up = [
        send(we_rows(peer(j)), relay_in.at[peer(j)], w_send.at[0, j], w_recv.at[0, peer(j)], {"layer": nxt})
        for j in range(1, feat_n)
    ]
    across = [
        send(relay_in.at[peer(j)], relay_mid.at[me_f], w_send.at[1, j], w_recv.at[1, me_f], {"feat": peer(j)})
        for j in range(1, feat_n)
    ]
    back = [
        send(relay_mid.at[peer(j)], wek.at[peer(j)], w_send.at[2, j], w_recv.at[2, peer(j)], {"layer": prv})
        for j in range(1, feat_n)
    ]
    direct = [
        send(we_rows(peer(j)), wek.at[me_f], w_send.at[3, j], w_recv.at[2, me_f], {"feat": peer(j)})
        for j in range(1, feat_n)
    ]

    def w_arrived(ref, stage, s):
        send(ref.at[s], ref.at[s], w_send.at[stage, 0], w_recv.at[stage, s], {"tok": other}).wait_recv()

    @pl.when(is_first)
    def _():
        for copy in first_up:
            copy.start()

    @pl.when(me_l == 1)
    def _():
        for j in range(1, feat_n):
            w_arrived(relay_in, 0, peer(j))
            across[j - 1].start()
        for j in range(1, feat_n):
            w_arrived(relay_mid, 1, peer(j))
            back[j - 1].start()

    @pl.when(has_prev)
    def _():
        for copy in direct:
            copy.start()

    ids = lax.broadcasted_iota(jnp.int32, (seq, 1), 0)
    lives = [ids < lengths[p] for p in streams]
    which = jnp.zeros((1, block), jnp.int32) + chosen[0, 0]
    modes = picks = jnp.zeros((1, block), jnp.int32)
    for b in range(mode_row.shape[1] // block):
        here = which == b
        modes = jnp.where(here, mode_row[:, b * block : (b + 1) * block], modes)
        picks = jnp.where(here, index_row[:, b * block : (b + 1) * block], picks)
    levels = jnp.zeros((1, block), F32)
    for v in range(entries):
        levels = jnp.where(picks == v, table[v], levels)
    mlp_col = column(scale_mlp[...])
    shift = bias[...]
    l_err.wait()
    err[...] = jnp.transpose(err_t[...])
    l_wv.wait()
    l_pat.wait()
    l_wo.wait()
    l_wd.wait()
    own_rows.wait()

    tok_v = [send(part_v.at[p], part_v2.at[p], t_send.at[0, p], t_recv.at[0, p], {"tok": other}) for p in streams]
    tok_e = [send(part_e.at[p], part_e2.at[p], t_send.at[1, p], t_recv.at[1, p], {"tok": other}) for p in streams]
    pending = []
    for p in streams:
        total = jnp.zeros((seq, kv), F32)
        for s in range(feat_n):
            @pl.when(jnp.logical_or(has_prev, me_f != s))
            def _():
                arrived(slots, xs_send, xs_recv, p, s)

            total += jnp.dot(slots[p, s], wv[pl.ds(s * width, width), :], preferred_element_type=F32)
        part_v[p] = total
        tok_v[p].start()
        tok_v[p].wait_recv()
        vals[p, me_f] = (part_v[p] + part_v2[p]).astype(BF16)
        pending += to_peers(vals, v_send, v_recv, p)

    q_ids = lax.broadcasted_iota(jnp.int32, (seq, seq), 0)
    k_ids = lax.broadcasted_iota(jnp.int32, (seq, seq), 1)
    for p in streams:
        keep = jnp.logical_and(k_ids <= q_ids, k_ids < lengths[p])
        total = jnp.zeros((seq, width), F32)
        for s in range(feat_n):
            await_peer(vals, v_send, v_recv, p, s)
            group = s * kv // head_dim
            d0 = s * kv % head_dim
            for u in range(per_group):
                weights = jnp.where(keep, pat[group * per_group + u, p].astype(F32), 0.0).astype(BF16)
                head = jnp.dot(weights, vals[p, s], preferred_element_type=F32).astype(BF16)
                total += lax.dot_general(head, wo[group, u, :, pl.ds(d0, kv)], NT, preferred_element_type=F32)

        @pl.when(has_prev)
        def _():
            x_up[p].wait_recv()

        if p == 0:
            for s in range(feat_n):
                @pl.when(me_f != s)
                def _():
                    w_arrived(wek, 2, s)

        middle = xbuf[p] + total
        normed_mlp = (middle * mlp_col[p * seq : (p + 1) * seq]).astype(BF16)
        for j in range(1, feat_n):
            e_out[p, j] = jnp.dot(normed_mlp, wek[peer(j)], preferred_element_type=F32).astype(BF16)
            copy = send(e_out.at[p, j], e_in.at[p, me_f], m_send.at[p, j], m_recv.at[p, me_f], {"feat": peer(j)})
            copy.start()
            pending.append(copy)
        part_e[p] = jnp.dot(normed_mlp, wek[me_f], preferred_element_type=F32)
        att[part(p), :] = middle + err[part(p), :]

    for p in streams:
        for s in range(feat_n):
            @pl.when(me_f != s)
            def _():
                arrived(e_in, m_send, m_recv, p, s)
                part_e[p] += e_in[p, s].astype(F32)

        tok_e[p].start()
        tok_e[p].wait_recv()
        preact = part_e[p] + part_e2[p] + shift
        active = jnp.maximum(preact, 0.0)
        clamped = jnp.where(modes == 1, levels, jnp.where(modes == 2, active * levels, active))
        new_feats = jnp.where(lives[p], clamped, 0.0).astype(BF16)
        feats[p, me_f] = new_feats
        pending += to_peers(feats, f_send, f_recv, p)
        feat_ref[part(p), :] = new_feats

    def acc_copy(p, t):
        return send(acc_out.at[p, t], acc_in.at[p, t], a_send.at[p, t], a_recv.at[p, t], {"layer": nxt})

    def norm_up(p, s):
        return send(nbuf.at[p], slots.at[p, me_f], ns_send.at[p, s], xs_recv.at[p, me_f], {"layer": nxt, "feat": s})

    @pl.when(has_next)
    def _():
        send(scale_attn, next_scale, one_send.at[0], one_recv.at[0], {"layer": nxt}).wait_recv()

    for p in streams:
        @pl.when(has_prev)
        def _():
            for t in range(1, layers):
                @pl.when(t >= me_l)
                def _():
                    acc_copy(p, t).wait_recv()
            att[part(p), :] += acc_in[p, me_l]

        total = att[part(p), :]
        for s in range(feat_n):
            await_peer(feats, f_send, f_recv, p, s)
            total += lax.dot_general(feats[p, s], wd[me_l, :, pl.ds(s * block, block)], NT, preferred_element_type=F32)
        att[part(p), :] = total

        @pl.when(has_next)
        def _():
            after = att[part(p), :]
            nbuf[p] = (after * column(next_scale[...])[p * seq : (p + 1) * seq]).astype(BF16)
            for s in range(feat_n):
                norm_up(p, s).start()
            xsend[p] = after
            x_up[p].start()

    @pl.when(has_next)
    def _():
        for p in streams:
            for t in range(1, layers):
                @pl.when(t > me_l)
                def _():
                    total = jnp.zeros((seq, width), F32)
                    for s in range(feat_n):
                        total += lax.dot_general(
                            feats[p, s], wd[t, :, pl.ds(s * block, block)], NT, preferred_element_type=F32
                        )
                    acc_out[p, t] = total

                    @pl.when(has_prev)
                    def _():
                        acc_out[p, t] += acc_in[p, t]

                    acc_copy(p, t).start()

    out_ref[...] = jnp.transpose(att[...])

    @pl.when(is_first)
    def _():
        for p in streams:
            for j in range(1, feat_n):
                send(
                    slots.at[p, me_f], slots.at[p, me_f], xs_send.at[p, j], xs_recv.at[p, me_f], {"tok": other}
                ).wait_send()
        for copy in first_up:
            copy.wait_send()

    @pl.when(me_l == 1)
    def _():
        for copy in across + back:
            copy.wait_send()

    @pl.when(has_prev)
    def _():
        scale_up.wait_send()
        for copy in direct:
            copy.wait_send()

    for copy in tok_v + tok_e + pending:
        copy.wait_send()

    @pl.when(has_next)
    def _():
        for p in streams:
            for s in range(feat_n):
                norm_up(p, s).wait_send()
            x_up[p].wait_send()
            for t in range(1, layers):
                @pl.when(t > me_l)
                def _():
                    acc_copy(p, t).wait_send()


def local(
    residual_in, attn_scale, mlp_scale, patterns, lengths, value_proj, out_proj, enc_weight, enc_bias,
    dec_weight, errors, clamp_mode, clamp_index, clamp_values, active_blocks,
):
    layers = lax.axis_size("layer")
    feat_n = lax.axis_size("feat")
    prompts, seq = patterns.shape[2], patterns.shape[3]
    head_dim, per_group = out_proj.shape[2], out_proj.shape[3]
    kv = value_proj.shape[3]
    rows, _, width = residual_in.shape
    block = enc_bias.shape[1]
    entries = clamp_values.shape[0]
    sizes = (layers, feat_n, seq, prompts, head_dim, per_group, kv, width, block, rows, entries)
    x_in = residual_in[:, 0, :].T
    err_in = errors[0, :, 0, :].T
    pat_in = patterns[0]
    wv_in = value_proj[0, 0]
    wo_in = jnp.transpose(out_proj[0, :, :, :, 0, :], (0, 2, 3, 1))
    we_in = enc_weight[0, 0]
    wd_in = jnp.transpose(dec_weight[0, :, :, 0, :], (0, 2, 1))
    smem = pl.BlockSpec(memory_space=pltpu.SMEM)
    vmem = pl.BlockSpec(memory_space=pltpu.VMEM)
    hbm = pl.BlockSpec(memory_space=pl.ANY)
    big = (x_in, err_in, pat_in, wv_in, wo_in, we_in, wd_in)
    dma = pltpu.SemaphoreType.DMA
    out_t, out_f = pl.pallas_call(
        functools.partial(kernel, sizes),
        out_shape=(
            jax.ShapeDtypeStruct((width, rows), F32),
            jax.ShapeDtypeStruct((rows, block), BF16),
        ),
        in_specs=[smem] * 3 + [vmem] * 5 + [hbm] * 7,
        out_specs=(vmem, vmem),
        scratch_shapes=[pltpu.VMEM(a.shape, a.dtype) for a in big]
        + [
            pltpu.VMEM((prompts, seq, width), F32),
            pltpu.VMEM((prompts, feat_n, seq, width), BF16),
            pltpu.VMEM((prompts, feat_n, seq, kv), BF16),
            pltpu.VMEM((prompts, feat_n, seq, block), BF16),
            pltpu.VMEM((prompts, seq, kv), F32),
            pltpu.VMEM((prompts, seq, kv), F32),
            pltpu.VMEM((prompts, seq, block), F32),
            pltpu.VMEM((prompts, seq, block), F32),
            pltpu.VMEM((prompts, feat_n, seq, block), BF16),
            pltpu.VMEM((prompts, feat_n, seq, block), BF16),
            pltpu.VMEM((1, rows), F32),
            pltpu.VMEM((prompts, seq, width), BF16),
            pltpu.VMEM((prompts, seq, width), F32),
            pltpu.VMEM((prompts, layers, seq, width), F32),
            pltpu.VMEM((prompts, layers, seq, width), F32),
            pltpu.VMEM((rows, width), F32),
            pltpu.VMEM((rows, width), F32),
        ]
        + [pltpu.VMEM((feat_n, width, block), BF16)] * 3
        + [dma((8,))]
        + [dma((prompts, feat_n))] * 9
        + [dma((2, prompts))] * 2
        + [dma((prompts,))] * 2
        + [dma((1,))] * 2
        + [dma((prompts, layers))] * 2
        + [dma((4, feat_n)), dma((3, feat_n))],
        compiler_params=pltpu.CompilerParams(collective_id=0, has_side_effects=True),
    )(lengths, clamp_values, active_blocks, attn_scale, mlp_scale, enc_bias, clamp_mode, clamp_index, *big)
    return out_t.T[None, :, None, :], out_f[None]


def solution(mesh):
    return jax.shard_map(
        local,
        mesh=mesh,
        in_specs=(
            P("groups", "tok", "feat"),
            P("layer", "groups"),
            P("layer", "groups"),
            P("layer", None, "groups", None, None),
            P("groups"),
            P("layer", "tok", None, "feat"),
            P("layer", None, None, None, "tok", "feat"),
            P("layer", "tok", None, "feat"),
            P("layer", "feat"),
            P("layer", None, None, "tok", "feat"),
            P("layer", "groups", "tok", "feat"),
            P("layer", "feat"),
            P("layer", "feat"),
            P(),
            P("layer", "feat"),
        ),
        out_specs=(P("layer", "groups", "tok", "feat"), P("layer", "groups", "feat")),
        check_vma=False,
    )
```

```python
import functools

import jax
import jax.numpy as jnp
from jax import lax
from jax.experimental import pallas as pl
from jax.experimental.pallas import tpu as pltpu
from jax.sharding import PartitionSpec as P

F32 = jnp.float32
BF16 = jnp.bfloat16
NT = (((1,), (1,)), ((), ()))


def column(row):
    rows = row.shape[1]
    return jnp.transpose(jnp.broadcast_to(row, (128, rows)))[:, 0:1]


def kernel(
    sizes,
    lengths, table, chosen,
    scale_attn, scale_mlp, bias, mode_row, index_row,
    x_in, err_in, pat_in, wv_in, wo_in, we_in, wd_in,
    out_ref, feat_ref,
    x_t, err_t, pat, wv, wo, we, wd,
    xbuf, slots, vals, feats, part_v, part_v2, part_e, part_e2, e_out, e_in,
    next_scale, nbuf, xsend, acc_in, acc_out, att, err, wek, relay_in, relay_mid,
    local_sem, xs_send, xs_recv, ns_send, v_send, v_recv, m_send, m_recv, f_send, f_recv,
    t_send, t_recv, up_send, up_recv, one_send, one_recv, a_send, a_recv,
    w_send, w_recv, b_send, b_recv,
):
    layers, feat_n, seq, prompts, head_dim, per_group, kv, width, block, rows, entries, shares = sizes
    me_g = lax.axis_index("groups")
    me_l = lax.axis_index("layer")
    me_f = lax.axis_index("feat")
    me_t = lax.axis_index("tok")
    has_next = me_l < layers - 1
    has_prev = me_l > 0
    is_first = jnp.logical_not(has_prev)
    other = 1 - me_t
    nxt = jnp.minimum(me_l + 1, layers - 1)
    prv = jnp.maximum(me_l - 1, 0)
    streams = range(prompts)

    loads = [
        pltpu.make_async_copy(src, dst, local_sem.at[i])
        for i, (src, dst) in enumerate(
            ((x_in, x_t), (we_in, we), (wv_in, wv), (pat_in, pat), (wo_in, wo), (wd_in, wd), (err_in, err_t))
        )
    ]
    for load in loads:
        load.start()
    l_x, l_we, l_wv, l_pat, l_wo, l_wd, l_err = loads

    barrier = pltpu.get_barrier_semaphore()
    mesh_id = pl.DeviceIdType.MESH
    pl.semaphore_signal(barrier, inc=1, device_id={"tok": other}, device_id_type=mesh_id)
    for j in range(1, feat_n):
        pl.semaphore_signal(barrier, inc=1, device_id={"feat": (me_f + j) % feat_n}, device_id_type=mesh_id)

    @pl.when(has_next)
    def _():
        for s in range(feat_n):
            pl.semaphore_signal(barrier, inc=1, device_id={"layer": nxt, "feat": s}, device_id_type=mesh_id)

    @pl.when(has_prev)
    def _():
        for s in range(feat_n):
            pl.semaphore_signal(barrier, inc=1, device_id={"layer": prv, "feat": s}, device_id_type=mesh_id)

    def send(src, dst, ss, rs, where):
        return pltpu.make_async_remote_copy(
            src_ref=src, dst_ref=dst, send_sem=ss, recv_sem=rs, device_id=where, device_id_type=mesh_id
        )

    def peer(j):
        return (me_f + j) % feat_n

    def part(p):
        return pl.ds(p * seq, seq)

    l_x.wait()
    x_rows = jnp.transpose(x_t[...])
    normed = (x_rows * column(scale_attn[...])).astype(BF16)

    @pl.when(is_first)
    def _():
        for p in streams:
            slots[p, me_f] = normed[p * seq : (p + 1) * seq]
            xbuf[p] = x_rows[p * seq : (p + 1) * seq]

    for g in range(1, shares):
        @pl.when(is_first)
        def _():
            pl.semaphore_signal(
                barrier, inc=1, device_id={"groups": (me_g + g) % shares, "layer": nxt}, device_id_type=mesh_id
            )

        @pl.when(me_l == 1)
        def _():
            pl.semaphore_signal(
                barrier, inc=1, device_id={"groups": (me_g + g) % shares, "layer": prv}, device_id_type=mesh_id
            )

    extra = (shares - 1) * (1 - jnp.minimum(me_l // 2, 1))
    neighbours = 1 + jnp.minimum(me_l, 1) + jnp.minimum(layers - 1 - me_l, 1)
    pl.semaphore_wait(barrier, feat_n * neighbours + extra)

    def to_peers(ref, ss, rs, p):
        copies = [
            send(ref.at[p, me_f], ref.at[p, me_f], ss.at[p, j], rs.at[p, me_f], {"feat": peer(j)})
            for j in range(1, feat_n)
        ]
        for copy in copies:
            copy.start()
        return copies

    def arrived(ref, ss, rs, p, s):
        send(ref.at[p, s], ref.at[p, s], ss.at[p, 0], rs.at[p, s], {"tok": other}).wait_recv()

    def await_peer(ref, ss, rs, p, s):
        @pl.when(me_f != s)
        def _():
            arrived(ref, ss, rs, p, s)

    @pl.when(is_first)
    def _():
        for p in streams:
            to_peers(slots, xs_send, xs_recv, p)

    scale_up = send(scale_attn, next_scale, one_send.at[0], one_recv.at[0], {"layer": prv})
    x_up = [send(xsend.at[p], xbuf.at[p], up_send.at[p], up_recv.at[p], {"layer": nxt}) for p in streams]

    @pl.when(has_prev)
    def _():
        scale_up.start()

    def we_rows(s):
        return we.at[pl.ds(pl.multiple_of(s * width, 16), width)]

    l_we.wait()
    own_rows = pltpu.make_async_copy(we_rows(me_f), wek.at[me_f], local_sem.at[7])
    own_rows.start()
    share = width // shares
    my_share = me_g if shares > 1 else 0
    front = pl.ds(0, share)
    first_up = [
        send(
            we.at[pl.ds(pl.multiple_of(peer(j) * width + my_share * share, 16), share)],
            relay_in.at[peer(j), front], w_send.at[0, j], w_recv.at[0, peer(j)], {"layer": nxt},
        )
        for j in range(1, feat_n)
    ]
    across = [
        send(
            relay_in.at[peer(j), front], relay_mid.at[me_f, front],
            w_send.at[1, j], w_recv.at[1, me_f], {"feat": peer(j)},
        )
        for j in range(1, feat_n)
    ]
    back = [
        [
            send(
                relay_mid.at[peer(j), front],
                wek.at[peer(j), pl.ds(pl.multiple_of(my_share * share, 16), share)],
                b_send.at[g, j], b_recv.at[my_share, peer(j)],
                {"layer": prv, "groups": (me_g + g) % shares} if g else {"layer": prv},
            )
            for g in range(shares)
        ]
        for j in range(1, feat_n)
    ]
    direct = [
        send(we_rows(peer(j)), wek.at[me_f], w_send.at[3, j], w_recv.at[2, me_f], {"feat": peer(j)})
        for j in range(1, feat_n)
    ]

    def w_arrived(ref, stage, s):
        part_ref = ref.at[s, front] if stage < 2 else ref.at[s]
        send(part_ref, part_ref, w_send.at[stage, 0], w_recv.at[stage, s], {"tok": other}).wait_recv()

    @pl.when(is_first)
    def _():
        for copy in first_up:
            copy.start()

    @pl.when(me_l == 1)
    def _():
        for j in range(1, feat_n):
            w_arrived(relay_in, 0, peer(j))
            across[j - 1].start()
        for j in range(1, feat_n):
            w_arrived(relay_mid, 1, peer(j))
            for copy in back[j - 1]:
                copy.start()

    @pl.when(has_prev)
    def _():
        for copy in direct:
            copy.start()

    ids = lax.broadcasted_iota(jnp.int32, (seq, 1), 0)
    lives = [ids < lengths[p] for p in streams]
    which = jnp.zeros((1, block), jnp.int32) + chosen[0, 0]
    modes = picks = jnp.zeros((1, block), jnp.int32)
    for b in range(mode_row.shape[1] // block):
        here = which == b
        modes = jnp.where(here, mode_row[:, b * block : (b + 1) * block], modes)
        picks = jnp.where(here, index_row[:, b * block : (b + 1) * block], picks)
    levels = jnp.zeros((1, block), F32)
    for v in range(entries):
        levels = jnp.where(picks == v, table[v], levels)
    mlp_col = column(scale_mlp[...])
    shift = bias[...]
    l_err.wait()
    err[...] = jnp.transpose(err_t[...])
    l_wv.wait()
    l_pat.wait()
    l_wo.wait()
    l_wd.wait()
    own_rows.wait()

    tok_v = [send(part_v.at[p], part_v2.at[p], t_send.at[0, p], t_recv.at[0, p], {"tok": other}) for p in streams]
    tok_e = [send(part_e.at[p], part_e2.at[p], t_send.at[1, p], t_recv.at[1, p], {"tok": other}) for p in streams]
    pending = []
    for p in streams:
        total = jnp.zeros((seq, kv), F32)
        for s in range(feat_n):
            @pl.when(jnp.logical_or(has_prev, me_f != s))
            def _():
                arrived(slots, xs_send, xs_recv, p, s)

            total += jnp.dot(slots[p, s], wv[pl.ds(s * width, width), :], preferred_element_type=F32)
        part_v[p] = total
        tok_v[p].start()
        tok_v[p].wait_recv()
        vals[p, me_f] = (part_v[p] + part_v2[p]).astype(BF16)
        pending += to_peers(vals, v_send, v_recv, p)

    q_ids = lax.broadcasted_iota(jnp.int32, (seq, seq), 0)
    k_ids = lax.broadcasted_iota(jnp.int32, (seq, seq), 1)
    for p in streams:
        keep = jnp.logical_and(k_ids <= q_ids, k_ids < lengths[p])
        total = jnp.zeros((seq, width), F32)
        for s in range(feat_n):
            await_peer(vals, v_send, v_recv, p, s)
            group = s * kv // head_dim
            d0 = s * kv % head_dim
            for u in range(per_group):
                weights = jnp.where(keep, pat[group * per_group + u, p].astype(F32), 0.0).astype(BF16)
                head = jnp.dot(weights, vals[p, s], preferred_element_type=F32).astype(BF16)
                total += lax.dot_general(head, wo[group, u, :, pl.ds(d0, kv)], NT, preferred_element_type=F32)

        @pl.when(has_prev)
        def _():
            x_up[p].wait_recv()

        if p == 0:
            for s in range(feat_n):
                @pl.when(jnp.logical_and(has_prev, me_f != s))
                def _():
                    w_arrived(wek, 2, s)

                @pl.when(jnp.logical_and(is_first, me_f != s))
                def _():
                    for g in range(shares):
                        here = wek.at[s, pl.ds(g * share, share)]
                        send(here, here, b_send.at[0, 0], b_recv.at[g, s], {"tok": other}).wait_recv()

        middle = xbuf[p] + total
        normed_mlp = (middle * mlp_col[p * seq : (p + 1) * seq]).astype(BF16)
        for j in range(1, feat_n):
            e_out[p, j] = jnp.dot(normed_mlp, wek[peer(j)], preferred_element_type=F32).astype(BF16)
            copy = send(e_out.at[p, j], e_in.at[p, me_f], m_send.at[p, j], m_recv.at[p, me_f], {"feat": peer(j)})
            copy.start()
            pending.append(copy)
        part_e[p] = jnp.dot(normed_mlp, wek[me_f], preferred_element_type=F32)
        att[part(p), :] = middle + err[part(p), :]

    for p in streams:
        for s in range(feat_n):
            @pl.when(me_f != s)
            def _():
                arrived(e_in, m_send, m_recv, p, s)
                part_e[p] += e_in[p, s].astype(F32)

        tok_e[p].start()
        tok_e[p].wait_recv()
        preact = part_e[p] + part_e2[p] + shift
        active = jnp.maximum(preact, 0.0)
        clamped = jnp.where(modes == 1, levels, jnp.where(modes == 2, active * levels, active))
        new_feats = jnp.where(lives[p], clamped, 0.0).astype(BF16)
        feats[p, me_f] = new_feats
        pending += to_peers(feats, f_send, f_recv, p)
        feat_ref[part(p), :] = new_feats

    def acc_copy(p, t):
        return send(acc_out.at[p, t], acc_in.at[p, t], a_send.at[p, t], a_recv.at[p, t], {"layer": nxt})

    def norm_up(p, s):
        return send(nbuf.at[p], slots.at[p, me_f], ns_send.at[p, s], xs_recv.at[p, me_f], {"layer": nxt, "feat": s})

    @pl.when(has_next)
    def _():
        send(scale_attn, next_scale, one_send.at[0], one_recv.at[0], {"layer": nxt}).wait_recv()

    for p in streams:
        @pl.when(has_prev)
        def _():
            for t in range(1, layers):
                @pl.when(t >= me_l)
                def _():
                    acc_copy(p, t).wait_recv()
            att[part(p), :] += acc_in[p, me_l]

        total = att[part(p), :]
        for s in range(feat_n):
            await_peer(feats, f_send, f_recv, p, s)
            total += lax.dot_general(feats[p, s], wd[me_l, :, pl.ds(s * block, block)], NT, preferred_element_type=F32)
        att[part(p), :] = total

        @pl.when(has_next)
        def _():
            after = att[part(p), :]
            nbuf[p] = (after * column(next_scale[...])[p * seq : (p + 1) * seq]).astype(BF16)
            for s in range(feat_n):
                norm_up(p, s).start()
            xsend[p] = after

    @pl.when(has_next)
    def _():
        for p in streams:
            x_up[p].start()
        for p in streams:
            for t in range(1, layers):
                @pl.when(t > me_l)
                def _():
                    total = jnp.zeros((seq, width), F32)
                    for s in range(feat_n):
                        total += lax.dot_general(
                            feats[p, s], wd[t, :, pl.ds(s * block, block)], NT, preferred_element_type=F32
                        )
                    acc_out[p, t] = total

                    @pl.when(has_prev)
                    def _():
                        acc_out[p, t] += acc_in[p, t]

                    acc_copy(p, t).start()

    out_ref[...] = jnp.transpose(att[...])

    @pl.when(is_first)
    def _():
        for p in streams:
            for j in range(1, feat_n):
                send(
                    slots.at[p, me_f], slots.at[p, me_f], xs_send.at[p, j], xs_recv.at[p, me_f], {"tok": other}
                ).wait_send()
        for copy in first_up:
            copy.wait_send()

    @pl.when(me_l == 1)
    def _():
        for copy in sum(back, across):
            copy.wait_send()

    @pl.when(has_prev)
    def _():
        scale_up.wait_send()
        for copy in direct:
            copy.wait_send()

    for copy in tok_v + tok_e + pending:
        copy.wait_send()

    @pl.when(has_next)
    def _():
        for p in streams:
            for s in range(feat_n):
                norm_up(p, s).wait_send()
            x_up[p].wait_send()
            for t in range(1, layers):
                @pl.when(t > me_l)
                def _():
                    acc_copy(p, t).wait_send()


def store(x_ref, f_ref, out_ref, feat_ref, sems):
    copies = [
        pltpu.make_async_copy(x_ref, out_ref, sems.at[0]),
        pltpu.make_async_copy(f_ref, feat_ref, sems.at[1]),
    ]
    for copy in copies:
        copy.start()
    for copy in copies:
        copy.wait()


def local(
    residual_in, attn_scale, mlp_scale, patterns, lengths, value_proj, out_proj, enc_weight, enc_bias,
    dec_weight, errors, clamp_mode, clamp_index, clamp_values, active_blocks,
):
    layers = lax.axis_size("layer")
    feat_n = lax.axis_size("feat")
    prompts, seq = patterns.shape[2], patterns.shape[3]
    head_dim, per_group = out_proj.shape[2], out_proj.shape[3]
    kv = value_proj.shape[3]
    rows, _, width = residual_in.shape
    block = enc_bias.shape[1]
    entries = clamp_values.shape[0]
    groups = lax.axis_size("groups")
    shares = groups if width % (16 * groups) == 0 else 1
    sizes = (layers, feat_n, seq, prompts, head_dim, per_group, kv, width, block, rows, entries, shares)
    x_in = residual_in[:, 0, :].T
    err_in = errors[0, :, 0, :].T
    pat_in = patterns[0]
    wv_in = value_proj[0, 0]
    wo_in = jnp.transpose(out_proj[0, :, :, :, 0, :], (0, 2, 3, 1))
    we_in = enc_weight[0, 0]
    wd_in = jnp.transpose(dec_weight[0, :, :, 0, :], (0, 2, 1))
    smem = pl.BlockSpec(memory_space=pltpu.SMEM)
    vmem = pl.BlockSpec(memory_space=pltpu.VMEM)
    hbm = pl.BlockSpec(memory_space=pl.ANY)
    big = (x_in, err_in, pat_in, wv_in, wo_in, we_in, wd_in)
    dma = pltpu.SemaphoreType.DMA
    out_t, out_f = pl.pallas_call(
        functools.partial(kernel, sizes),
        out_shape=(
            jax.ShapeDtypeStruct((width, rows), F32),
            jax.ShapeDtypeStruct((rows, block), BF16),
        ),
        in_specs=[smem] * 3 + [vmem] * 5 + [hbm] * 7,
        out_specs=(vmem, vmem),
        scratch_shapes=[pltpu.VMEM(a.shape, a.dtype) for a in big]
        + [
            pltpu.VMEM((prompts, seq, width), F32),
            pltpu.VMEM((prompts, feat_n, seq, width), BF16),
            pltpu.VMEM((prompts, feat_n, seq, kv), BF16),
            pltpu.VMEM((prompts, feat_n, seq, block), BF16),
            pltpu.VMEM((prompts, seq, kv), F32),
            pltpu.VMEM((prompts, seq, kv), F32),
            pltpu.VMEM((prompts, seq, block), F32),
            pltpu.VMEM((prompts, seq, block), F32),
            pltpu.VMEM((prompts, feat_n, seq, block), BF16),
            pltpu.VMEM((prompts, feat_n, seq, block), BF16),
            pltpu.VMEM((1, rows), F32),
            pltpu.VMEM((prompts, seq, width), BF16),
            pltpu.VMEM((prompts, seq, width), F32),
            pltpu.VMEM((prompts, layers, seq, width), F32),
            pltpu.VMEM((prompts, layers, seq, width), F32),
            pltpu.VMEM((rows, width), F32),
            pltpu.VMEM((rows, width), F32),
        ]
        + [pltpu.VMEM((feat_n, width, block), BF16)] * 3
        + [dma((8,))]
        + [dma((prompts, feat_n))] * 9
        + [dma((2, prompts))] * 2
        + [dma((prompts,))] * 2
        + [dma((1,))] * 2
        + [dma((prompts, layers))] * 2
        + [dma((4, feat_n)), dma((3, feat_n))]
        + [dma((shares, feat_n))] * 2,
        compiler_params=pltpu.CompilerParams(collective_id=0, has_side_effects=True),
    )(lengths, clamp_values, active_blocks, attn_scale, mlp_scale, enc_bias, clamp_mode, clamp_index, *big)
    out_t, out_f = pl.pallas_call(
        store,
        out_shape=(
            jax.ShapeDtypeStruct((width, rows), F32),
            jax.ShapeDtypeStruct((rows, block), BF16),
        ),
        in_specs=[vmem, vmem],
        out_specs=(hbm, hbm),
        scratch_shapes=[dma((2,))],
    )(out_t, out_f)
    return out_t.T[None, :, None, :], out_f[None]


def solution(mesh):
    return jax.shard_map(
        local,
        mesh=mesh,
        in_specs=(
            P("groups", "tok", "feat"),
            P("layer", "groups"),
            P("layer", "groups"),
            P("layer", None, "groups", None, None),
            P("groups"),
            P("layer", "tok", None, "feat"),
            P("layer", None, None, None, "tok", "feat"),
            P("layer", "tok", None, "feat"),
            P("layer", "feat"),
            P("layer", None, None, "tok", "feat"),
            P("layer", "groups", "tok", "feat"),
            P("layer", "feat"),
            P("layer", "feat"),
            P(),
            P("layer", "feat"),
        ),
        out_specs=(P("layer", "groups", "tok", "feat"), P("layer", "groups", "feat")),
        check_vma=False,
    )
```
